512 devices in a mesh: dp: 32 (over y, x, core), tensor: 16 (over z).
Axes of the slice: x: 4, y: 4, z: 16, core: 2. Of those that a mesh axis runs over, the one named last changes fastest.
Arguments:
- tokens: bfloat16 [16384, 8192], P('dp', 'tensor'), may hold values from -6 to 6
- row_adapter_index: int32 [16384, 1], P('dp'), may hold values from 0 to 255; in each aligned block of 512 rows (0 to 511, 512 to 1023, ...) at most 4 rows name the same one
- adapter_storage_slot: int32 [256], replicated, may hold values from 0 to 255, each once
- key_value_base_weight: bfloat16 [8192, 2, 1024], P('tensor'), may hold values from -0.09375 to 0.09375
- adapter_down_weight: bfloat16 [256, 8192, 128], P('dp', 'tensor'), may hold values from -0.0625 to 0.0625
- adapter_up_weight: bfloat16 [256, 2, 64, 1024], P('dp', None, None, 'tensor'), may hold values from -0.75 to 0.75
Outputs:
- key_value: bfloat16 [16384, 2, 1024], P('dp', None, 'tensor')
The draws below stay inside these ranges and needn't reach their ends.
Inputs may be any that keep to these rules, and one draw needn't show every extreme that they name: `row_adapter_index`: within the rows of one index of dp no adapter is named by more than 4 rows, a bound that some block reaches. `adapter_storage_slot`: A permutation of the slots.
All inputs are finite; a program needn't handle non-finite values.
Results may differ from the reference program's by a relative error of at most 0.0034.
Values may be sent and summed in bfloat16 or wider, within the bound.
A program may use at most 64 MiB of HBM per device.

```python
import math
import jax
import jax.numpy as jnp
import numpy as np
from jax import lax

MODEL_WIDTH = 8192
KEY_VALUE_WIDTH = 1024
ADAPTER_RANK = 64
TOK_DEV = 512
ADAPTER_TOTAL = 256
CAP = 4
TOKENS = 16384
N_DP = 32
N_TENSOR = 16


def spiked(drawn, key, source, target, blocks, factor):
    def block_of(position):
        return (jnp.arange(drawn.shape[position]) // (drawn.shape[position] // blocks)).reshape((-1,) + (1,) * (drawn.ndim - 1 - position))

    first = jax.random.permutation(key, blocks)[block_of(target)]
    other_side = (block_of(target) + blocks // 2) % blocks
    return jnp.where((block_of(source) == first) | (block_of(source) == other_side), factor * drawn, drawn)


def shard_levels(stream_key, extent, pieces, smallest, largest):
    loudness = 1.0
    for position, parts in pieces:
        draws = jax.random.uniform(jax.random.fold_in(jax.random.fold_in(stream_key, 6), position), (parts,), jnp.float32, smallest / len(pieces), largest / len(pieces))
        loudness = loudness * jnp.repeat(jnp.exp(draws), extent[position] // parts).reshape((-1,) + (1,) * (len(extent) - 1 - position))
    return loudness


def routed_block(stream_key, own, number, rows, amount, top, most, skew):
    ranking = jax.random.permutation(stream_key, amount)
    packed, common = portions_of(amount, rows * top, most, skew, True), portions_of(amount, rows * top, most, skew, False)
    places = jnp.arange(amount)

    def named(lengths, offset_by):
        used = int((lengths > 0).sum())
        fixed = max(1, used // 4)
        passed = fixed + (places - fixed + offset_by * (used - fixed)) % max(1, amount - fixed)
        return jnp.zeros((amount,), jnp.int32).at[ranking[jnp.where(places < fixed, places, passed)]].set(jnp.asarray(lengths, jnp.int32))

    lengths = jnp.where(number % 4 == 0, named(packed, number // 4), named(common, number - number // 4 - 1))
    mixed = jax.random.permutation(jax.random.fold_in(own, 3), amount)
    source_of, sink = mixed[0:amount // 2 * 2:2], mixed[1:amount // 2 * 2:2]
    margin = jnp.minimum(lengths[source_of] - 1, most - lengths[sink]) // 2
    margin = jnp.where((source_of == ranking[0]) | (sink == ranking[0]) | (lengths[sink] == 0), 0, jnp.maximum(margin, 0))
    passed = jax.random.randint(jax.random.fold_in(own, 4), (amount // 2,), 0, 1 << 20) % (margin + 1)
    lengths = lengths.at[source_of].add(-passed).at[sink].add(passed)
    items = jnp.searchsorted(jnp.cumsum(lengths), jnp.arange(rows * top), side="right").astype(jnp.int32)
    grid = items.reshape(top, rows).T
    grid = grid[jax.random.permutation(jax.random.fold_in(own, 1), rows)]
    offset_by = jax.random.randint(jax.random.fold_in(own, 2), (rows, 1), 0, top)
    return jnp.take_along_axis(grid, (jnp.arange(top)[None, :] + offset_by) % top, axis=1)


def portions_of(count, total, limit, slope, full):
    weights = [(1 << 20) // math.isqrt(standing ** slope) + 1 for standing in range(1, count + 1)]
    largest = limit if full else min(limit, max(-(-total // count), total * weights[0] // sum(weights)))
    least = 1 if total - largest >= count - 1 else 0
    given, surplus = [largest] + [least] * (count - 1), total - largest - least * (count - 1)
    while surplus > 0:
        candidates = [i for i in range(1, count) if given[i] < largest] or [i for i in range(1, count) if given[i] < limit]
        whole, remaining = sum([weights[i] for i in candidates]), surplus
        for i in candidates:
            addition = min(limit - given[i], max(1, remaining * weights[i] // whole), surplus)
            given[i] = given[i] + addition
            surplus = surplus - addition
    return np.array(given)


def scatter_about(own_key, shape, scale, limit, shards=(), held_as=jnp.bfloat16):
    factor_of = shard_levels(own_key, shape, shards, -0.22, 0.18) if shards else 1.0
    array = jax.random.normal(own_key, shape, jnp.float32) * scale * factor_of
    return jnp.minimum(jnp.maximum(array, -limit), limit).astype(held_as)


def heavy_noise(rng, shape, width, limit, shards, heavy, held_as=jnp.bfloat16):
    array = width * jax.random.normal(rng, shape, jnp.float32)
    if shards:
        array = array * shard_levels(rng, shape, shards, -0.22, 0.18)
    return jnp.clip(spiked(array, jax.random.fold_in(rng, 3), *heavy), -limit, limit).astype(held_as)


def setup_inputs(seed: int = 0) -> dict:
    seeds = jax.random.split(jax.random.key(seed), 7)
    tokens = scatter_about(seeds[0], (TOKENS, MODEL_WIDTH), 1.0, 6.0, ((0, 32), (1, 16)))
    row_adapter_index_keys = jax.random.split(jax.random.fold_in(seeds[1], 1), TOKENS // TOK_DEV)
    row_adapter_index_turns = jax.random.permutation(jax.random.fold_in(seeds[1], 3), TOKENS // TOK_DEV)
    row_adapter_index = jax.vmap(lambda own, number: routed_block(jax.random.fold_in(seeds[1], 2), own, number, TOK_DEV, ADAPTER_TOTAL, 1, CAP, 2))(row_adapter_index_keys, row_adapter_index_turns).reshape((TOKENS, 1))
    adapter_storage_slot = jax.random.permutation(seeds[2], ADAPTER_TOTAL).astype(jnp.int32)
    key_value_base_weight = heavy_noise(seeds[3], (MODEL_WIDTH, 2, KEY_VALUE_WIDTH), MODEL_WIDTH ** -0.5, 0.09375, ((0, 16),), (0, 2, 16, 2.0))
    adapter_down_weight = scatter_about(seeds[4], (ADAPTER_TOTAL, MODEL_WIDTH, 2 * ADAPTER_RANK), MODEL_WIDTH ** -0.5, 0.0625, ((0, 32), (1, 16)))
    adapter_up_weight = scatter_about(seeds[5], (ADAPTER_TOTAL, 2, ADAPTER_RANK, KEY_VALUE_WIDTH), ADAPTER_RANK ** -0.5, 0.75, ((0, 32), (3, 16)))
    return {"tokens": tokens, "row_adapter_index": row_adapter_index, "adapter_storage_slot": adapter_storage_slot, "key_value_base_weight": key_value_base_weight, "adapter_down_weight": adapter_down_weight, "adapter_up_weight": adapter_up_weight}


adapter_scale = 0.5


def reference(tokens, row_adapter_index, adapter_storage_slot, key_value_base_weight, adapter_down_weight, adapter_up_weight):
    count_rows, full_width = tokens.shape
    shard_width = full_width // N_TENSOR
    blocked_x = tokens.reshape(count_rows, N_TENSOR, shard_width)
    blocked_w = key_value_base_weight.reshape(N_TENSOR, shard_width, 2 * KEY_VALUE_WIDTH)

    def add_block(summed, block_index):
        piece_x = lax.dynamic_index_in_dim(blocked_x, block_index, 1, keepdims=False)
        piece_w = lax.dynamic_index_in_dim(blocked_w, block_index, 0, keepdims=False)
        product = jnp.dot(piece_x, piece_w, preferred_element_type=jnp.float32)
        return summed + product, None

    base, unused = lax.scan(add_block, jnp.zeros((count_rows, 2 * KEY_VALUE_WIDTH), jnp.float32),
                            jnp.arange(N_TENSOR, dtype=jnp.int32))
    base = base.reshape(count_rows, 2, KEY_VALUE_WIDTH)

    adapter_of = row_adapter_index[:, 0]
    order_rows = jnp.argsort(adapter_of, stable=True).astype(jnp.int32)
    counts = jnp.zeros((ADAPTER_TOTAL,), jnp.int32).at[adapter_of].add(1)
    starts = jnp.cumsum(counts) - counts
    most_rows = N_DP * CAP
    offsets = jnp.arange(most_rows, dtype=jnp.int32)

    def one_adapter(adapter):
        is_used = offsets < counts[adapter]
        chosen_rows = order_rows[jnp.minimum(starts[adapter] + offsets, count_rows - 1)]
        storage_device = adapter_storage_slot[adapter]
        reduced_rows = jnp.dot(tokens[chosen_rows], adapter_down_weight[storage_device], preferred_element_type=jnp.float32).astype(jnp.bfloat16)
        reduced_rows = lax.optimization_barrier(reduced_rows)
        reduced_rows = reduced_rows.astype(jnp.float32).reshape(most_rows, 2, ADAPTER_RANK)
        adapter_delta = jnp.einsum("ave,vef->avf", reduced_rows, adapter_up_weight[storage_device].astype(jnp.float32))
        adapter_delta = (adapter_scale * adapter_delta).astype(jnp.bfloat16)
        adapter_delta = jnp.where(is_used[:, None, None], adapter_delta, jnp.zeros_like(adapter_delta))
        return chosen_rows, adapter_delta

    picked_all, updates = lax.map(one_adapter, jnp.arange(ADAPTER_TOTAL, dtype=jnp.int32))
    updates = lax.optimization_barrier(updates)
    summed = jnp.zeros((count_rows, 2, KEY_VALUE_WIDTH), jnp.float32).at[picked_all.reshape(-1)].add(
        updates.reshape(-1, 2, KEY_VALUE_WIDTH).astype(jnp.float32))
    return (base + summed).astype(jnp.bfloat16)
```

```python
import functools

import jax
import jax.numpy as jnp
from jax import lax
from jax.experimental import pallas as pl
from jax.experimental.pallas import tpu as pltpu
from jax.sharding import PartitionSpec as P

MESH = pl.DeviceIdType.MESH
BF = jnp.bfloat16
F32 = jnp.float32
I32 = jnp.int32
I16 = jnp.int16

Z = 16
SIDE = 4
DP = 32
ROWS = 512
SLOTS = 8
CAP = 4
PAIR = SLOTS * CAP
CHUNK = 2 * PAIR
Q = 4
QR = ROWS // Q
QX = QR + 16
LEVELS = 32000.0
SCALE = 0.5

PLAN = (
    ("S", 0), ("B", 0), ("L", 0), ("L", 1), ("B", 1), ("L", 2), ("L", 3), ("B", 2), ("L", 4), ("L", 5),
    ("B", 3), ("L", 6), ("L", 7), ("B", 4), ("LF", 0), ("G", 0), ("B", 5), ("GR", 0), ("U", 1), ("U", 2),
    ("U", 3), ("U", 4), ("B", 6), ("U", 5), ("U", 6), ("U", 7), ("U", 8), ("B", 7), ("BF", 0), ("H", 0),
)
REACH = 4
PAIRS = ((8, -7), (7, -6), (6, -5), (5, -3), (3, -2), (2, -1), (1, 0), (4, -4))


def kernel(
    x_hbm, idx_hbm, slot_hbm, w_hbm, down_hbm, up_hbm, out_ref,
    x_ref, idx_ref, slot_ref, w_ref, up_ref,
    perm, outbox, inbox, downcat, upbig, updates, returned, gath,
    b_send_r, b_send_l, b_recv_r, b_recv_l, own, base_t,
    l_send, l_recv, l_own,
    sem_in, sem_down, sem_br, sem_bl, sem_l, sem_g, sem_a, sem_ret,
    sent_br, sent_bl, sent_l, sent_g, sent_a, sent_ret,
):
    me = lax.axis_index("dp")
    z = lax.axis_index("tensor")
    core = lax.rem(me, 2)
    chip = me // 2
    y, x = chip // SIDE, lax.rem(chip, SIDE)
    right, left = lax.rem(z + 1, Z), lax.rem(z + Z - 1, Z)

    def mod_z(v):
        return lax.rem(v + 2 * Z, Z)

    def chip_at(q, sign):
        qy, qx = q // SIDE, lax.rem(q, SIDE)
        return lax.rem(y + sign * qy + SIDE, SIDE) * SIDE + lax.rem(x + sign * qx + SIDE, SIDE)

    def remote(src, dst, sent, got, dp, zz):
        return pltpu.make_async_remote_copy(
            src_ref=src, dst_ref=dst, send_sem=sent, recv_sem=got,
            device_id=(dp, zz), device_id_type=MESH,
        )

    barrier = pltpu.get_barrier_semaphore()

    @pl.loop(1, DP)
    def _(i):
        pl.semaphore_signal(
            barrier, inc=1, device_id=(lax.rem(me + i, DP), z), device_id_type=MESH
        )

    for k in range(1, REACH + 1):
        for zz in (mod_z(z + k), mod_z(z - k)):
            pl.semaphore_signal(barrier, inc=1, device_id=(me, zz), device_id_type=MESH)

    fetch = [
        pltpu.make_async_copy(src, dst, sem_in.at[i])
        for i, (src, dst) in enumerate(
            ((idx_hbm, idx_ref), (slot_hbm, slot_ref), (x_hbm, x_ref), (w_hbm, w_ref), (up_hbm, up_ref))
        )
    ]
    fetch_down = [
        pltpu.make_async_copy(down_hbm.at[e], downcat.at[:, e * 128:(e + 1) * 128], sem_down.at[e])
        for e in range(SLOTS)
    ]
    for copy in fetch + fetch_down:
        copy.start()

    fetch[0].wait()
    fetch[1].wait()
    adapters = idx_ref[...]
    names = slot_ref.shape[1]
    onehot = (lax.broadcasted_iota(I32, (names, ROWS), 0) == adapters).astype(F32).astype(BF)
    before = (
        lax.broadcasted_iota(I32, (ROWS, ROWS), 0) < lax.broadcasted_iota(I32, (ROWS, ROWS), 1)
    ).astype(F32).astype(BF)
    earlier = jnp.dot(onehot, before, preferred_element_type=F32)
    position = jnp.sum(earlier * onehot.astype(F32), axis=0, keepdims=True)
    slots = jnp.broadcast_to(slot_ref[...].astype(F32), (8, names)).astype(BF)
    storage = jnp.dot(slots, onehot, preferred_element_type=F32)[0:1, :]
    target = (storage * CAP + position).astype(I32)
    fetch[2].wait()
    tokens = x_ref[...]
    blk = 256
    for i in range(DP * PAIR // blk):
        part = (lax.broadcasted_iota(I32, (blk, ROWS), 0) + i * blk == target).astype(F32).astype(BF)
        perm[i * blk:(i + 1) * blk, :] = part
        outbox[i * blk:(i + 1) * blk, :] = jnp.dot(part, tokens, preferred_element_type=F32).astype(BF)

    def weight_of(c):
        tile = pl.ds(pl.multiple_of((c // 2) * 128, 128), 128)
        k, v = w_ref[:, 0, tile], w_ref[:, 1, tile]
        low = jnp.concatenate([k[:, :64], v[:, :64]], axis=1)
        high = jnp.concatenate([k[:, 64:], v[:, 64:]], axis=1)
        odd = jnp.broadcast_to(lax.rem(c, 2), low.shape) == 1
        return jnp.where(odd, high, low)

    def partial_of(c):
        return jnp.dot(x_ref[...], weight_of(c), preferred_element_type=F32)

    def encode(v, ref):
        top = jnp.max(jnp.abs(v), axis=0, keepdims=True)
        power = jnp.ceil(jnp.log(top + 1e-30) * 1.4426950408889634)
        code = jnp.round(v * (jnp.exp2(-power) * LEVELS))
        ref[0:QR, :] = code.astype(I32).astype(I16)
        ref[QR:QX, :] = jnp.broadcast_to(power, (16, 128)).astype(I32).astype(I16)

    def decode(ref):
        power = ref[QR:QX, :].astype(I32).astype(F32)[0:1, :]
        return ref[0:QR, :].astype(I32).astype(F32) * (jnp.exp2(power) * (1.0 / LEVELS))

    def base_step(s, send=True):
        part = partial_of(mod_z(z + 8 - s)) if send != "only" else None
        for b in range(Q):
            if send != "only":
                v = part[b * QR:(b + 1) * QR, :]
                if s > 0:
                    remote(b_send_r.at[s - 1, b], b_recv_r.at[s - 1, b], sent_br, sem_br.at[s - 1, b], me, right).wait_recv()
                    v = v + decode(b_recv_r.at[s - 1, b])
                encode(v, b_send_r.at[s, b])
            if send:
                remote(b_send_r.at[s, b], b_recv_r.at[s, b], sent_br, sem_br.at[s, b], me, right).start()
        part = partial_of(mod_z(z + 9 + s)) if send != "only" else None
        if s == 7:
            own[...] = part
            return
        for b in range(Q):
            if send != "only":
                v = part[b * QR:(b + 1) * QR, :]
                if s > 0:
                    remote(b_send_l.at[s - 1, b], b_recv_l.at[s - 1, b], sent_bl, sem_bl.at[s - 1, b], me, left).wait_recv()
                    v = v + decode(b_recv_l.at[s - 1, b])
                encode(v, b_send_l.at[s, b])
            if send:
                remote(b_send_l.at[s, b], b_recv_l.at[s, b], sent_bl, sem_bl.at[s, b], me, left).start()

    def base_final():
        for b in range(Q):
            remote(b_send_r.at[7, b], b_recv_r.at[7, b], sent_br, sem_br.at[7, b], me, right).wait_recv()
            remote(b_send_l.at[6, b], b_recv_l.at[6, b], sent_bl, sem_bl.at[6, b], me, left).wait_recv()
            rows = slice(b * QR, (b + 1) * QR)
            total = own[rows, :] + decode(b_recv_r.at[7, b]) + decode(b_recv_l.at[6, b])
            base_t[:, rows] = total.T

    def send_tokens():
        for k in range(Z):
            q = mod_z(z + PAIRS[k // 2][k % 2])
            there = chip_at(q, -1)
            mine = pl.ds(pl.multiple_of(q * CHUNK + core * PAIR, PAIR), PAIR)
            got = sem_a.at[q * 2 + core]
            for c in range(2):
                d = there * 2 + c
                src = outbox.at[pl.ds(pl.multiple_of(d * PAIR, PAIR), PAIR), :]

                @pl.when(d != me)
                def _():
                    remote(src, inbox.at[mine, :], sent_a, got, d, z).start()

                @pl.when(d == me)
                def _():
                    pltpu.make_async_copy(src, inbox.at[mine, :], got).start()

    def wait_tokens(q):
        for c in range(2):
            mine = inbox.at[pl.ds(pl.multiple_of(q * CHUNK + c * PAIR, PAIR), PAIR), :]
            pltpu.make_async_copy(mine, mine, sem_a.at[q * 2 + c]).wait()

    def chunk_rows(q):
        return pl.ds(pl.multiple_of(q * CHUNK, CHUNK), CHUNK)

    def adapter_of(rows):
        return lax.rem(lax.broadcasted_iota(I32, (rows, 128), 0), PAIR) // CAP

    def lora_send(i, dp_z, slot):
        return remote(l_send.at[i], l_recv.at[slot], sent_l, sem_l.at[slot], me, dp_z)

    def lora_step(s):
        offsets = PAIRS[s]
        chunks = [mod_z(z + o) for o in offsets]
        for q in chunks:
            wait_tokens(q)
        if s == 0:
            for copy in fetch_down:
                copy.wait()
        rows = jnp.concatenate([inbox[chunk_rows(q), :] for q in chunks], axis=0)
        full = jnp.dot(rows, downcat[...], preferred_element_type=F32)
        which = adapter_of(2 * CHUNK)
        piece = jnp.zeros((2 * CHUNK, 128), F32)
        for e in range(SLOTS):
            piece = jnp.where(which == e, full[:, e * 128:(e + 1) * 128], piece)
        for k, o in enumerate(offsets):
            mine = piece[k * CHUNK:(k + 1) * CHUNK, :]
            i = 2 * s + k
            far, sign = abs(o), (1 if o > 0 else -1)
            if o == 0:
                l_own[...] = mine
                continue
            if far > REACH:
                to, slot = sign * (far - REACH), (8 if o > 0 else 12) + far - REACH - 1
            else:
                to, slot = o, (0 if o > 0 else 4) + far - 1
            if far == REACH:
                for j in range(4 if o > 0 else 3):
                    got = (8 if o > 0 else 12) + j
                    lora_send(i, mod_z(z - sign * (j + 1)), got).wait_recv()
                    mine = mine + l_recv[got].astype(F32)
            l_send[i] = mine.astype(BF)
            lora_send(i, mod_z(z + to), slot).start()

    def lora_final():
        total = l_own[...]
        for slot in range(8):
            lora_send(0, mod_z(z + 1), slot).wait_recv()
            total = total + l_recv[slot].astype(F32)
        gath[z] = total.astype(BF)

    def gather_send(c, to, got):
        return remote(gath.at[c], gath.at[c], sent_g, sem_g.at[got], me, mod_z(z + to))

    def gather_wait(k):
        c = mod_z(z + k)
        gather_send(c, 1, (-k - 1) if k < 0 else 7 + k).wait_recv()

    def gather_first():
        for k in (4, 3, 2, 1):
            gather_send(z, k, k - 1).start()
            gather_send(z, -k, 7 + k).start()
        update_of([0])

    def gather_relay():
        gather_wait(-REACH)
        for k in (4, 3, 2, 1):
            gather_send(mod_z(z - REACH), k, k + REACH - 1).start()
        gather_wait(REACH)
        for k in (3, 2, 1):
            gather_send(mod_z(z + REACH), -k, 7 + k + REACH).start()

    def give_back(c):
        who = chip_at(c, 1)
        to = returned.at[pl.ds(pl.multiple_of(me * PAIR, PAIR), PAIR), :]
        for k in range(2):
            d = who * 2 + k
            src = updates.at[c, k * PAIR:(k + 1) * PAIR, :]

            @pl.when(d != me)
            def _():
                remote(src, to, sent_ret, sem_ret.at[me], d, z).start()

            @pl.when(d == me)
            def _():
                pltpu.make_async_copy(src, to, sem_ret.at[me]).start()

    def gather_step(k):
        offsets = [-k, k] if k < 8 else [-8]
        for o in offsets:
            if abs(o) != REACH:
                gather_wait(o)
        update_of(offsets)

    def update_of(offsets):
        chunks = [mod_z(z + o) for o in offsets]
        shrunk = [gath[c] for c in chunks]
        shrunk = jnp.concatenate(shrunk, axis=0) if len(chunks) > 1 else shrunk[0]
        which = adapter_of(CHUNK * len(chunks))
        spread = jnp.concatenate(
            [jnp.where(which == e, shrunk.astype(F32), 0.0).astype(BF) for e in range(SLOTS)], axis=1
        )
        delta = (SCALE * jnp.dot(spread, upbig[...], preferred_element_type=F32)).astype(BF)
        for i, c in enumerate(chunks):
            updates[c] = delta[i * CHUNK:(i + 1) * CHUNK, :]
            give_back(c)

    def finish():
        @pl.loop(0, DP)
        def _(i):
            part = returned.at[pl.ds(pl.multiple_of(i * PAIR, PAIR), PAIR), :]
            pltpu.make_async_copy(part, part, sem_ret.at[i]).wait()

        update_t = lax.dot_general(
            returned[...], perm[...], (((0,), (0,)), ((), ())), preferred_element_type=F32
        )
        out_ref[...] = (base_t[...] + update_t).astype(BF)

    def prepare():
        fetch[4].wait()
        for e in range(SLOTS):
            nothing = jnp.zeros((64, 64), BF)
            upbig[e * 128:e * 128 + 64, :] = jnp.concatenate([up_ref[e, 0], nothing], axis=1)
            upbig[e * 128 + 64:(e + 1) * 128, :] = jnp.concatenate([nothing, up_ref[e, 1]], axis=1)

    fetch[3].wait()
    base_step(0, False)
    pl.semaphore_wait(barrier, DP - 1 + 2 * REACH)
    for name, step in PLAN:
        if name == "S":
            send_tokens()
            prepare()
        elif name == "BF":
            base_final()
        elif name == "LF":
            lora_final()
        elif name == "H":
            finish()
        elif name == "B":
            base_step(step, True if step else "only")
        elif name == "L":
            lora_step(step)
        elif name == "G":
            gather_first()
        elif name == "GR":
            gather_relay()
        else:
            gather_step(step)

    def drain(ref, sem):
        pltpu.make_async_copy(ref, ref, sem).wait()

    drain(b_send_r, sent_br)
    drain(b_send_l, sent_bl)
    drain(l_send.at[0:15], sent_l)
    drain(gath.at[0:15], sent_g)
    drain(inbox.at[0:(DP - 1) * PAIR, :], sent_a)
    drain(returned.at[0:(DP - 1) * PAIR, :], sent_ret)


def per_device(tokens, row_adapter_index, storage_slot, base_weight, down, up):
    vmem = pl.BlockSpec(memory_space=pltpu.VMEM)
    dma = pltpu.SemaphoreType.DMA
    out = pl.pallas_call(
        kernel,
        out_shape=jax.ShapeDtypeStruct((128, ROWS), BF),
        in_specs=[pl.BlockSpec(memory_space=pltpu.HBM)] * 6,
        out_specs=vmem,
        scratch_shapes=[
            pltpu.VMEM((ROWS, 512), BF),
            pltpu.VMEM((1, ROWS), I32),
            pltpu.VMEM((1, storage_slot.shape[0]), I32),
            pltpu.VMEM(base_weight.shape, BF),
            pltpu.VMEM(up.shape, BF),
            pltpu.VMEM((DP * PAIR, ROWS), BF),
            pltpu.VMEM((DP * PAIR, 512), BF),
            pltpu.VMEM((DP * PAIR, 512), BF),
            pltpu.VMEM((512, SLOTS * 128), BF),
            pltpu.VMEM((SLOTS * 128, 128), BF),
            pltpu.VMEM((Z, CHUNK, 128), BF),
            pltpu.VMEM((DP * PAIR, 128), BF),
            pltpu.VMEM((Z, CHUNK, 128), BF),
            pltpu.VMEM((8, Q, QX, 128), I16),
            pltpu.VMEM((7, Q, QX, 128), I16),
            pltpu.VMEM((8, Q, QX, 128), I16),
            pltpu.VMEM((7, Q, QX, 128), I16),
            pltpu.VMEM((ROWS, 128), F32),
            pltpu.VMEM((128, ROWS), F32),
            pltpu.VMEM((Z, CHUNK, 128), BF),
            pltpu.VMEM((15, CHUNK, 128), BF),
            pltpu.VMEM((CHUNK, 128), F32),
            dma((5,)), dma((SLOTS,)), dma((8, Q)), dma((7, Q)), dma((15,)), dma((15,)), dma((DP,)), dma((DP,)),
            dma, dma, dma, dma, dma, dma,
        ],
        compiler_params=pltpu.CompilerParams(
            collective_id=0, has_side_effects=True, vmem_limit_bytes=60 << 20
        ),
    )(
        tokens,
        row_adapter_index.reshape(1, ROWS),
        storage_slot.reshape(1, -1),
        base_weight,
        down,
        up,
    )
    return out.reshape(2, 64, ROWS).transpose(2, 0, 1)


def solution(mesh):
    placed = (
        P("dp", "tensor"),
        P("dp", None),
        P(),
        P("tensor", None, None),
        P("dp", "tensor", None),
        P("dp", None, None, "tensor"),
    )
    return jax.shard_map(
        per_device, mesh=mesh, in_specs=placed, out_specs=P("dp", None, "tensor"), check_vma=False
    )
```

```python
import functools

import jax
import jax.numpy as jnp
from jax import lax
from jax.experimental import pallas as pl
from jax.experimental.pallas import tpu as pltpu
from jax.sharding import PartitionSpec as P

MESH = pl.DeviceIdType.MESH
BF = jnp.bfloat16
F32 = jnp.float32
I32 = jnp.int32
I16 = jnp.int16

Z = 16
SIDE = 4
DP = 32
ROWS = 512
SLOTS = 8
CAP = 4
PAIR = SLOTS * CAP
CHUNK = 2 * PAIR
Q = 4
QR = ROWS // Q
HEAD = 16
LEVELS = 32000.0
FINE = 256.0
SCALE = 0.5

PLAN = (('S', 0), ('S', 1), ('B', 0), ('S', 2), ('S', 3), ('L', 0), ('L', 1), ('B', 1), ('S', 4), ('S', 5), ('L', 2), ('L', 3), ('B', 2), ('S', 6), ('S', 7), ('L', 4), ('L', 5), ('B', 3), ('L', 6), ('L', 7), ('B', 4), ('LF', 0), ('G', 0), ('B', 5), ('GR', 0), ('U', 1), ('U', 2), ('U', 3), ('U', 4), ('B', 6), ('U', 5), ('U', 6), ('U', 7), ('U', 8), ('B', 7), ('BF', 0), ('H', 0))
REACH = 4
PAIRS = ((8, -7), (7, -6), (6, -5), (5, -3), (3, -2), (4, -4), (2, -1), (1, 0))


def kernel(
    x_hbm, idx_hbm, slot_hbm, w_hbm, down_hbm, up_hbm, out_ref,
    x_ref, idx_ref, slot_ref, w_ref, up_ref, w_all,
    perm, outbox, inbox, downcat, upbig, updates, returned, gath,
    b_send_r, b_send_l, b_recv_r, b_recv_l, part_r, part_l, top_r, top_l, base_t,
    l_send, l_recv, l_own,
    sem_in, sem_down, sem_br, sem_bl, sem_l, sem_g, sem_a, sem_ret,
    sent_br, sent_bl, sent_l, sent_g, sent_a, sent_ret,
):
    me = lax.axis_index("dp")
    z = lax.axis_index("tensor")
    core = lax.rem(me, 2)
    chip = me // 2
    y, x = chip // SIDE, lax.rem(chip, SIDE)
    right, left = lax.rem(z + 1, Z), lax.rem(z + Z - 1, Z)

    def mod_z(v):
        return lax.rem(v + 2 * Z, Z)

    def chip_at(q, sign):
        qy, qx = q // SIDE, lax.rem(q, SIDE)
        return lax.rem(y + sign * qy + SIDE, SIDE) * SIDE + lax.rem(x + sign * qx + SIDE, SIDE)

    def remote(src, dst, sent, got, dp, zz):
        return pltpu.make_async_remote_copy(
            src_ref=src, dst_ref=dst, send_sem=sent, recv_sem=got,
            device_id=(dp, zz), device_id_type=MESH,
        )

    barrier = pltpu.get_barrier_semaphore()

    @pl.loop(1, DP)
    def _(i):
        pl.semaphore_signal(
            barrier, inc=1, device_id=(lax.rem(me + i, DP), z), device_id_type=MESH
        )

    for k in range(1, REACH + 1):
        for zz in (mod_z(z + k), mod_z(z - k)):
            pl.semaphore_signal(barrier, inc=1, device_id=(me, zz), device_id_type=MESH)

    fetch = [
        pltpu.make_async_copy(src, dst, sem_in.at[i])
        for i, (src, dst) in enumerate(
            ((idx_hbm, idx_ref), (slot_hbm, slot_ref), (x_hbm, x_ref), (w_hbm, w_ref), (up_hbm, up_ref))
        )
    ]
    fetch_down = [
        pltpu.make_async_copy(down_hbm.at[e], downcat.at[:, e * 128:(e + 1) * 128], sem_down.at[e])
        for e in range(SLOTS)
    ]
    for copy in fetch + fetch_down:
        copy.start()

    fetch[0].wait()
    fetch[1].wait()
    adapters = idx_ref[...]
    names = slot_ref.shape[1]
    onehot = (lax.broadcasted_iota(I32, (names, ROWS), 0) == adapters).astype(F32).astype(BF)
    before = (
        lax.broadcasted_iota(I32, (ROWS, ROWS), 0) < lax.broadcasted_iota(I32, (ROWS, ROWS), 1)
    ).astype(F32).astype(BF)
    earlier = jnp.dot(onehot, before, preferred_element_type=F32)
    position = jnp.sum(earlier * onehot.astype(F32), axis=0, keepdims=True)
    slots = jnp.broadcast_to(slot_ref[...].astype(F32), (8, names)).astype(BF)
    storage = jnp.dot(slots, onehot, preferred_element_type=F32)[0:1, :]
    target = (storage * CAP + position).astype(I32)
    fetch[2].wait()
    tokens = x_ref[...]
    blk = 256
    for i in range(DP * PAIR // blk):
        part = (lax.broadcasted_iota(I32, (blk, ROWS), 0) + i * blk == target).astype(F32).astype(BF)
        perm[i * blk:(i + 1) * blk, :] = part
        outbox[i * blk:(i + 1) * blk, :] = jnp.dot(part, tokens, preferred_element_type=F32).astype(BF)

    def arrange_weights():
        first = lax.broadcasted_iota(I32, (512, 128), 1) < 64
        for m in range(Z // 2):
            pair = w_ref[:, :, m * 128:(m + 1) * 128].astype(F32)
            k, v = pair[:, 0, :], pair[:, 1, :]
            w_all[2 * m] = jnp.where(first, k, pltpu.roll(v, 64, 1)).astype(BF)
            w_all[2 * m + 1] = jnp.where(first, pltpu.roll(k, 64, 1), v).astype(BF)

    rings = (
        (b_send_r, b_recv_r, sent_br, sem_br, part_r, top_r, right, 8),
        (b_send_l, b_recv_l, sent_bl, sem_bl, part_l, top_l, left, 7),
    )

    def base_products(s):
        weights = jnp.concatenate([w_all[mod_z(z + 8 - s)], w_all[mod_z(z + 9 + s)]], axis=1)
        both = jnp.dot(x_ref[...], weights, preferred_element_type=F32)
        for i, ring in enumerate(rings):
            part = both[:, i * 128:(i + 1) * 128]
            ring[4][...] = part
            ring[5][...] = jnp.broadcast_to(jnp.max(jnp.abs(part), axis=0, keepdims=True), (8, 128))

    def block_rows(b):
        return slice(HEAD + b * QR, HEAD + (b + 1) * QR)

    def base_copy(ring, s, b):
        send, recv, sent, got, _, _, to, _ = ring
        rows = slice(0, HEAD + QR) if b == 0 else block_rows(b)
        return remote(send.at[s, rows, :], recv.at[s, rows, :], sent, got.at[s, b], me, to)

    def power_in(recv, s):
        return recv[s, 0:HEAD, :].astype(I32).astype(F32)[0:1, :] * (1.0 / FINE)

    def base_step(s, send=True):
        held = [None, None]
        for b in range(Q):
            for i, ring in enumerate(rings):
                out, recv, _, _, part, top, _, steps = ring
                if s >= steps:
                    continue
                if send != "only":
                    if s > 0:
                        base_copy(ring, s - 1, b).wait_recv()
                    if b == 0:
                        bound = top[0:1, :] + 1e-30
                        if s > 0:
                            before_scale = jnp.exp2(power_in(recv, s - 1))
                            bound = bound + before_scale
                        power = jnp.ceil(jnp.log(bound) * (FINE * 1.4426950408889634))
                        out[s, 0:HEAD, :] = jnp.broadcast_to(power, (HEAD, 128)).astype(I32).astype(I16)
                        scale = jnp.exp2(power * (-1.0 / FINE)) * LEVELS
                        held[i] = (scale, before_scale * scale * (1.0 / LEVELS) if s > 0 else None)
                    scale, ratio = held[i]
                    v = part[b * QR:(b + 1) * QR, :] * scale
                    if s > 0:
                        v = v + recv[s - 1, block_rows(b), :].astype(I32).astype(F32) * ratio
                    out[s, block_rows(b), :] = jnp.round(v).astype(I32).astype(I16)
                if send:
                    base_copy(ring, s, b).start()
        if send and s < 7:
            base_products(s + 1)

    def base_final():
        scales = [None, None]
        for b in range(Q):
            rows = slice(b * QR, (b + 1) * QR)
            total = part_l[rows, :]
            for i, ring in enumerate(rings):
                last = ring[7] - 1
                base_copy(ring, last, b).wait_recv()
                if b == 0:
                    scales[i] = jnp.exp2(power_in(ring[1], last)) * (1.0 / LEVELS)
                total = total + ring[1][last, block_rows(b), :].astype(I32).astype(F32) * scales[i]
            base_t[:, rows] = total.T

    def send_tokens(step):
        for offset in PAIRS[step]:
            q = mod_z(z + offset)
            there = chip_at(q, -1)
            mine = pl.ds(pl.multiple_of(q * CHUNK + core * PAIR, PAIR), PAIR)
            got = sem_a.at[q * 2 + core]
            for c in range(2):
                d = there * 2 + c
                src = outbox.at[pl.ds(pl.multiple_of(d * PAIR, PAIR), PAIR), :]

                @pl.when(d != me)
                def _():
                    remote(src, inbox.at[mine, :], sent_a, got, d, z).start()

                @pl.when(d == me)
                def _():
                    pltpu.make_async_copy(src, inbox.at[mine, :], got).start()

    def wait_tokens(q):
        for c in range(2):
            mine = inbox.at[pl.ds(pl.multiple_of(q * CHUNK + c * PAIR, PAIR), PAIR), :]
            pltpu.make_async_copy(mine, mine, sem_a.at[q * 2 + c]).wait()

    def chunk_rows(q):
        return pl.ds(pl.multiple_of(q * CHUNK, CHUNK), CHUNK)

    def adapter_of(rows):
        return lax.rem(lax.broadcasted_iota(I32, (rows, 128), 0), PAIR) // CAP

    def lora_send(i, dp_z, slot):
        return remote(l_send.at[i], l_recv.at[slot], sent_l, sem_l.at[slot], me, dp_z)

    def lora_step(s):
        offsets = PAIRS[s]
        chunks = [mod_z(z + o) for o in offsets]
        for q in chunks:
            wait_tokens(q)
        if s == 0:
            for copy in fetch_down:
                copy.wait()
        rows = jnp.concatenate([inbox[chunk_rows(q), :] for q in chunks], axis=0)
        full = jnp.dot(rows, downcat[...], preferred_element_type=F32)
        which = adapter_of(2 * CHUNK)
        piece = jnp.zeros((2 * CHUNK, 128), F32)
        for e in range(SLOTS):
            piece = jnp.where(which == e, full[:, e * 128:(e + 1) * 128], piece)
        for k, o in enumerate(offsets):
            mine = piece[k * CHUNK:(k + 1) * CHUNK, :]
            i = 2 * s + k
            far, sign = abs(o), (1 if o > 0 else -1)
            if o == 0:
                l_own[...] = mine
                continue
            if far > REACH:
                to, slot = sign * (far - REACH), (8 if o > 0 else 12) + far - REACH - 1
            else:
                to, slot = o, (0 if o > 0 else 4) + far - 1
            if far == REACH:
                for j in range(4 if o > 0 else 3):
                    got = (8 if o > 0 else 12) + j
                    lora_send(i, mod_z(z - sign * (j + 1)), got).wait_recv()
                    mine = mine + l_recv[got].astype(F32)
            l_send[i] = mine.astype(BF)
            lora_send(i, mod_z(z + to), slot).start()

    def lora_final():
        total = l_own[...]
        for slot in range(8):
            lora_send(0, mod_z(z + 1), slot).wait_recv()
            total = total + l_recv[slot].astype(F32)
        gath[z] = total.astype(BF)

    def gather_send(c, to, got):
        return remote(gath.at[c], gath.at[c], sent_g, sem_g.at[got], me, mod_z(z + to))

    def gather_wait(k):
        c = mod_z(z + k)
        gather_send(c, 1, (-k - 1) if k < 0 else 7 + k).wait_recv()

    def gather_first():
        for k in (4, 3, 2, 1):
            gather_send(z, k, k - 1).start()
            gather_send(z, -k, 7 + k).start()
        update_of([0])

    def gather_relay():
        gather_wait(-REACH)
        for k in (4, 3, 2, 1):
            gather_send(mod_z(z - REACH), k, k + REACH - 1).start()
        gather_wait(REACH)
        for k in (3, 2, 1):
            gather_send(mod_z(z + REACH), -k, 7 + k + REACH).start()

    def give_back(c):
        who = chip_at(c, 1)
        to = returned.at[pl.ds(pl.multiple_of(me * PAIR, PAIR), PAIR), :]
        for k in range(2):
            d = who * 2 + k
            src = updates.at[c, k * PAIR:(k + 1) * PAIR, :]

            @pl.when(d != me)
            def _():
                remote(src, to, sent_ret, sem_ret.at[me], d, z).start()

            @pl.when(d == me)
            def _():
                pltpu.make_async_copy(src, to, sem_ret.at[me]).start()

    def gather_step(k):
        offsets = [-k, k] if k < 8 else [-8]
        for o in offsets:
            if abs(o) != REACH:
                gather_wait(o)
        update_of(offsets)

    def update_of(offsets):
        chunks = [mod_z(z + o) for o in offsets]
        shrunk = [gath[c] for c in chunks]
        shrunk = jnp.concatenate(shrunk, axis=0) if len(chunks) > 1 else shrunk[0]
        which = adapter_of(CHUNK * len(chunks))
        spread = jnp.concatenate(
            [jnp.where(which == e, shrunk.astype(F32), 0.0).astype(BF) for e in range(SLOTS)], axis=1
        )
        delta = (SCALE * jnp.dot(spread, upbig[...], preferred_element_type=F32)).astype(BF)
        for i, c in enumerate(chunks):
            updates[c] = delta[i * CHUNK:(i + 1) * CHUNK, :]
            give_back(c)

    def finish():
        @pl.loop(0, DP)
        def _(i):
            part = returned.at[pl.ds(pl.multiple_of(i * PAIR, PAIR), PAIR), :]
            pltpu.make_async_copy(part, part, sem_ret.at[i]).wait()

        update_t = lax.dot_general(
            returned[...], perm[...], (((0,), (0,)), ((), ())), preferred_element_type=F32
        )
        out_ref[...] = (base_t[...] + update_t).astype(BF)

    def prepare():
        fetch[4].wait()
        for e in range(SLOTS):
            nothing = jnp.zeros((64, 64), BF)
            upbig[e * 128:e * 128 + 64, :] = jnp.concatenate([up_ref[e, 0], nothing], axis=1)
            upbig[e * 128 + 64:(e + 1) * 128, :] = jnp.concatenate([nothing, up_ref[e, 1]], axis=1)

    pl.semaphore_wait(barrier, DP - 1 + 2 * REACH)
    for name, step in PLAN:
        if name == "S":
            send_tokens(step)
            if step == 7:
                prepare()
        elif name == "BF":
            base_final()
        elif name == "LF":
            lora_final()
        elif name == "H":
            finish()
        elif name == "B":
            if step == 0:
                fetch[3].wait()
                arrange_weights()
                base_products(0)
            base_step(step)
        elif name == "L":
            lora_step(step)
        elif name == "G":
            gather_first()
        elif name == "GR":
            gather_relay()
        else:
            gather_step(step)

    def drain(ref, sem):
        pltpu.make_async_copy(ref, ref, sem).wait()

    drain(b_send_r, sent_br)
    drain(b_send_l, sent_bl)
    drain(l_send.at[0:15], sent_l)
    drain(gath.at[0:15], sent_g)
    drain(inbox.at[0:(DP - 1) * PAIR, :], sent_a)
    drain(returned.at[0:(DP - 1) * PAIR, :], sent_ret)


def per_device(tokens, row_adapter_index, storage_slot, base_weight, down, up):
    vmem = pl.BlockSpec(memory_space=pltpu.VMEM)
    dma = pltpu.SemaphoreType.DMA
    out = pl.pallas_call(
        kernel,
        out_shape=jax.ShapeDtypeStruct((128, ROWS), BF),
        in_specs=[pl.BlockSpec(memory_space=pltpu.HBM)] * 6,
        out_specs=vmem,
        scratch_shapes=[
            pltpu.VMEM((ROWS, 512), BF),
            pltpu.VMEM((1, ROWS), I32),
            pltpu.VMEM((1, storage_slot.shape[0]), I32),
            pltpu.VMEM(base_weight.shape, BF),
            pltpu.VMEM(up.shape, BF),
            pltpu.VMEM((Z, 512, 128), BF),
            pltpu.VMEM((DP * PAIR, ROWS), BF),
            pltpu.VMEM((DP * PAIR, 512), BF),
            pltpu.VMEM((DP * PAIR, 512), BF),
            pltpu.VMEM((512, SLOTS * 128), BF),
            pltpu.VMEM((SLOTS * 128, 128), BF),
            pltpu.VMEM((Z, CHUNK, 128), BF),
            pltpu.VMEM((DP * PAIR, 128), BF),
            pltpu.VMEM((Z, CHUNK, 128), BF),
            pltpu.VMEM((8, HEAD + ROWS, 128), I16),
            pltpu.VMEM((7, HEAD + ROWS, 128), I16),
            pltpu.VMEM((8, HEAD + ROWS, 128), I16),
            pltpu.VMEM((7, HEAD + ROWS, 128), I16),
            pltpu.VMEM((ROWS, 128), F32),
            pltpu.VMEM((ROWS, 128), F32),
            pltpu.VMEM((8, 128), F32),
            pltpu.VMEM((8, 128), F32),
            pltpu.VMEM((128, ROWS), F32),
            pltpu.VMEM((Z, CHUNK, 128), BF),
            pltpu.VMEM((15, CHUNK, 128), BF),
            pltpu.VMEM((CHUNK, 128), F32),
            dma((5,)), dma((SLOTS,)), dma((8, Q)), dma((7, Q)), dma((15,)), dma((15,)), dma((DP,)), dma((DP,)),
            dma, dma, dma, dma, dma, dma,
        ],
        compiler_params=pltpu.CompilerParams(
            collective_id=0, has_side_effects=True, vmem_limit_bytes=60 << 20
        ),
    )(
        tokens,
        row_adapter_index.reshape(1, ROWS),
        storage_slot.reshape(1, -1),
        base_weight,
        down,
        up,
    )
    return out.reshape(2, 64, ROWS).transpose(2, 0, 1)


def solution(mesh):
    placed = (
        P("dp", "tensor"),
        P("dp", None),
        P(),
        P("tensor", None, None),
        P("dp", "tensor", None),
        P("dp", None, None, "tensor"),
    )
    return jax.shard_map(
        per_device, mesh=mesh, in_specs=placed, out_specs=P("dp", None, "tensor"), check_vma=False
    )
```
